128 devices in a mesh: sph: 16 (over y_hi, x, core), grp: 8 (over z, y_lo).
Axes of the slice: x: 4, y: 4 (y_hi: 2, y_lo: 2; y = y_hi * 2 + y_lo), z: 4, core: 2. Of those that a mesh axis runs over, the one named last changes fastest.
Arguments:
- pixel_features: bfloat16 [131072, 512], P(('sph', 'grp')), may hold values from -6 to 6
- tier_one_codes: bfloat16 [8192, 512], P(('sph', 'grp')), may hold values from -6 to 6
- tier_two_codes: bfloat16 [512, 512], P(('sph', 'grp')), may hold values from -6 to 6
- tier_three_codes: bfloat16 [32, 512], P('sph'), may hold values from -6 to 6
- tier_one_picks: int32 [8192, 16], P(('sph', 'grp')), may hold values from 0 to 8191, as said below
- tier_two_picks: int32 [8192, 16], P(('sph', 'grp')), may hold values from 0 to 511, as said below
- tier_three_picks: int32 [8192, 16], P(('sph', 'grp')), may hold values from 0 to 31, as said below
- probe_matrix: bfloat16 [3, 512, 512], replicated, may hold values from -0.25 to 0.25
- address_matrix: bfloat16 [3, 512, 512], replicated, may hold values from -0.25 to 0.25
- content_matrix: bfloat16 [3, 512, 512], replicated, may hold values from -0.25 to 0.25
- merge_matrix: bfloat16 [3, 512, 512], replicated, may hold values from -0.25 to 0.25
- expand_matrix: bfloat16 [3, 512, 1024], replicated, may hold values from -0.25 to 0.25
- shrink_matrix: bfloat16 [3, 1024, 512], replicated, may hold values from -0.1875 to 0.1875
- rescale_factors: float32 [3, 3, 512], replicated, may hold values from 0.25 to 1.75
- logit_scaling: float32 [3, 8], replicated, may hold values from 0.5 to 2
Outputs:
- encoded: bfloat16 [131072, 512], P(('sph', 'grp'))
The draws below stay inside these ranges and needn't reach their ends.
Inputs may be any that keep to these rules, and one draw needn't show every extreme that they name: `tier_one_picks`: entry 0 of block b's list is b, its own level-one parent; every entry lies within 64 of b. `tier_two_picks`: entry 0 of block b's list is b // 16, its level-two parent; every entry lies in the same aligned run of 32 level-two latents as entry 0. `tier_three_picks`: entry 0 of block b's list is b // 256, its level-three parent.
All inputs are finite; a program needn't handle non-finite values.
Results may differ from the reference program's by a relative error of at most 0.01.
Values may be sent and summed in bfloat16 or wider, within the bound.
No kernel may reach another device: no remote copies, remote signals or barrier semaphores. Data moves between devices by JAX's collectives and lax.ppermute only.
A program may use at most 128 MiB of HBM per device.

```python
import math
import jax
import jax.numpy as jnp
from jax import lax

D = 512
HEADS_ALL = 8
FFL = 1024
LIST = 16
BLK_DEV = 64
NFINE = 131072
LAT1 = 8192
LAT2 = 512
LAT3 = 32
GROUP2 = 32


def draw_tier_one_picks(key, part):
    anchor = jnp.arange(LAT1, dtype=jnp.int32)[:, None]
    offsets = jax.random.randint(key, (LAT1, LIST), -BLK_DEV, BLK_DEV + 1, dtype=jnp.int32)
    offsets = jnp.concatenate([jnp.zeros((LAT1, 1), jnp.int32), offsets[:, 1:]], axis=1)
    return jnp.clip(anchor + offsets, 0, LAT1 - 1).astype(jnp.int32)


def draw_tier_two_picks(key, part):
    parent = (jnp.arange(LAT1, dtype=jnp.int32) // 16)[:, None]
    start_row = parent // GROUP2 * GROUP2
    picks = jax.random.randint(key, (LAT1, LIST), 0, GROUP2, dtype=jnp.int32) + start_row
    return jnp.concatenate([parent, picks[:, 1:]], axis=1).astype(jnp.int32)


def draw_tier_three_picks(key, part):
    parent = (jnp.arange(LAT1, dtype=jnp.int32) // 256)[:, None]
    picks = jax.random.randint(key, (LAT1, LIST), 0, LAT3, dtype=jnp.int32)
    return jnp.concatenate([parent, picks[:, 1:]], axis=1).astype(jnp.int32)


def levels(own_key, dims, shards, smallest, largest):
    gain = 1.0
    for axis_at, blocks in shards:
        steps = jax.random.uniform(jax.random.fold_in(jax.random.fold_in(own_key, 6), axis_at), (blocks,), jnp.float32, smallest / len(shards), largest / len(shards))
        gain = gain * jnp.repeat(jnp.exp(steps), dims[axis_at] // blocks).reshape((-1,) + (1,) * (len(dims) - 1 - axis_at))
    return gain


def normal_values(own_key, dims, scale, limit, cuts=(), held_as=jnp.bfloat16):
    values = scale * jax.random.normal(own_key, dims, jnp.float32)
    if cuts:
        values = values * levels(own_key, dims, cuts, -0.22, 0.18)
    return jnp.clip(values, -limit, limit).astype(held_as)


def setup_inputs(seed: int = 0) -> dict:
    streams_of = jax.random.split(jax.random.key(seed), 16)
    return {
        "pixel_features": normal_values(streams_of[0], (NFINE, D), 1.0, 6.0, ((0, 128),)),
        "tier_one_codes": normal_values(streams_of[1], (LAT1, D), 1.0, 6.0, ((0, 128),)),
        "tier_two_codes": normal_values(streams_of[2], (LAT2, D), 1.0, 6.0, ((0, 128),)),
        "tier_three_codes": normal_values(streams_of[3], (LAT3, D), 1.0, 6.0, ((0, 16),)),
        "tier_one_picks": draw_tier_one_picks(jax.random.fold_in(streams_of[15], 71), 0),
        "tier_two_picks": draw_tier_two_picks(jax.random.fold_in(streams_of[15], 71), 0),
        "tier_three_picks": draw_tier_three_picks(jax.random.fold_in(streams_of[15], 71), 0),
        "probe_matrix": normal_values(streams_of[7], (3, D, D), D ** -0.5, 0.25),
        "address_matrix": normal_values(streams_of[8], (3, D, D), D ** -0.5, 0.25),
        "content_matrix": normal_values(streams_of[9], (3, D, D), D ** -0.5, 0.25),
        "merge_matrix": normal_values(streams_of[10], (3, D, D), D ** -0.5, 0.25),
        "expand_matrix": normal_values(streams_of[11], (3, D, FFL), D ** -0.5, 0.25),
        "shrink_matrix": normal_values(streams_of[12], (3, FFL, D), FFL ** -0.5, 0.1875),
        "rescale_factors": jnp.clip(1.0 + 0.15 * jax.random.normal(streams_of[13], (3, 3, D), jnp.float32), 0.25, 1.75),
        "logit_scaling": jnp.clip(jnp.exp(jax.random.uniform(streams_of[14], (3, HEADS_ALL), jnp.float32, math.log(0.5), math.log(2.0))), 0.5, 2.0),
    }


eps = 1e-06

def normalize(values_in, gain_vec):
    return values_in * lax.rsqrt(lax.optimization_barrier(jnp.mean(values_in * values_in, axis=-1, keepdims=True)) + eps) * gain_vec

def per_head(values_in):
    dims_shape = values_in.shape
    grouped = values_in.reshape(dims_shape[:-1] + (HEADS_ALL, dims_shape[-1] // HEADS_ALL))
    grouped = grouped * lax.rsqrt(lax.optimization_barrier(jnp.mean(grouped * grouped, axis=-1, keepdims=True)) + eps)
    return grouped.reshape(dims_shape)

def refresh(latent, tier_ordinal, expand_matrix, shrink_matrix, rescale_factors):
    running_features = latent.astype(jnp.float32)
    mlp_in = normalize(running_features, rescale_factors[tier_ordinal, 1]).astype(jnp.bfloat16)
    hidden = jax.nn.silu(jnp.dot(mlp_in, expand_matrix[tier_ordinal], preferred_element_type=jnp.float32)).astype(jnp.bfloat16)
    renewed = (running_features + jnp.dot(hidden, shrink_matrix[tier_ordinal], preferred_element_type=jnp.float32)).astype(jnp.bfloat16)
    return lax.optimization_barrier(renewed)

def project(renewed, tier_ordinal, address_matrix, content_matrix, rescale_factors):
    kv_in = normalize(renewed.astype(jnp.float32), rescale_factors[tier_ordinal, 2]).astype(jnp.bfloat16)
    key_part = per_head(jnp.dot(kv_in, address_matrix[tier_ordinal], preferred_element_type=jnp.float32)).astype(jnp.bfloat16)
    value_part = jnp.dot(kv_in, content_matrix[tier_ordinal], preferred_element_type=jnp.float32).astype(jnp.bfloat16)
    return jnp.concatenate([key_part, value_part], axis=1)

def mix_across_tiers(running_features, gather_entries, tier_positions, tier_ordinal, probe_matrix, merge_matrix, rescale_factors, logit_scaling):
    row_count, feature = running_features.shape
    blocks = tier_positions.shape[0]
    group_dimension = feature // HEADS_ALL
    normed = normalize(running_features, rescale_factors[tier_ordinal, 0]).astype(jnp.bfloat16)
    queries = per_head(jnp.dot(normed, probe_matrix[tier_ordinal], preferred_element_type=jnp.float32)).astype(jnp.bfloat16)
    queries = queries.reshape(blocks, row_count // blocks, HEADS_ALL, group_dimension)
    chosen = jnp.take(gather_entries, tier_positions, axis=0)
    key_part = chosen[:, :, :feature].reshape(blocks, -1, HEADS_ALL, group_dimension)
    value_part = chosen[:, :, feature:].reshape(blocks, -1, HEADS_ALL, group_dimension)
    affinity_logits = jnp.einsum('bihd,bjhd->bhij', queries.astype(jnp.float32), key_part.astype(jnp.float32))
    affinity_logits = affinity_logits * (logit_scaling[tier_ordinal] / math.sqrt(group_dimension))[None, :, None, None]
    weights = jnp.exp(affinity_logits)
    weights = (weights / lax.optimization_barrier(jnp.sum(weights, axis=-1, keepdims=True))).astype(jnp.bfloat16)
    mixture = jnp.einsum('bhij,bjhd->bihd', weights.astype(jnp.float32), value_part.astype(jnp.float32))
    mixture = mixture.reshape(row_count, feature).astype(jnp.bfloat16)
    return running_features + jnp.dot(mixture, merge_matrix[tier_ordinal], preferred_element_type=jnp.float32)

def reference(pixel_features, tier_one_codes, tier_two_codes, tier_three_codes, tier_one_picks, tier_two_picks, tier_three_picks, probe_matrix, address_matrix, content_matrix, merge_matrix, expand_matrix, shrink_matrix, rescale_factors, logit_scaling):
    tables = []
    for tier_ordinal, latent in enumerate((tier_one_codes, tier_two_codes, tier_three_codes)):
        renewed = refresh(latent, tier_ordinal, expand_matrix, shrink_matrix, rescale_factors)
        tables.append(project(renewed, tier_ordinal, address_matrix, content_matrix, rescale_factors))
    group_count = NFINE // 4096
    states = pixel_features.astype(jnp.float32).reshape(group_count, 4096, D)
    first = tier_one_picks.reshape(group_count, 256, LIST)
    second = tier_two_picks.reshape(group_count, 256, LIST)
    third = tier_three_picks.reshape(group_count, 256, LIST)

    def one_group(packed):
        running_features, index_one, index_two, index_three = packed
        for tier_ordinal, (gather_entries, tier_positions) in enumerate(zip(tables, (index_one, index_two, index_three))):
            running_features = mix_across_tiers(running_features, gather_entries, tier_positions, tier_ordinal, probe_matrix, merge_matrix, rescale_factors, logit_scaling)
        return running_features.astype(jnp.bfloat16)
    result = lax.map(one_group, (states, first, second, third))
    return result.reshape(NFINE, D)
```

```python
import functools
import math

import jax
import jax.numpy as jnp
from jax import lax
from jax.experimental import pallas as pl
from jax.experimental.pallas import tpu as pltpu
from jax.sharding import PartitionSpec as P

eps = 1e-06
both = ("sph", "grp")
f32 = jnp.float32
bf16 = jnp.bfloat16
masked = -8192.0
log2e = 1.4426950408889634
heads = 8
head = 64
width = 512
listed = 16
tile = 256
in_vmem = pl.BlockSpec(memory_space=pltpu.VMEM)
in_smem = pl.BlockSpec(memory_space=pltpu.SMEM)
anywhere = pl.BlockSpec(memory_space=pl.ANY)


def iota(shape, dim):
    return lax.broadcasted_iota(jnp.int32, shape, dim)


def dot(left, right):
    return jnp.dot(left, right, preferred_element_type=f32)


def dot_t(left, right):
    return lax.dot_general(left, right, (((1,), (1,)), ((), ())), preferred_element_type=f32)


def head_mean_matrix():
    same = (iota((256, 256), 0) // head) == (iota((256, 256), 1) // head)
    return jnp.where(same, 1.0 / head, 0.0).astype(bf16)


def head_mean(values, averaging):
    squares = (values * values).astype(bf16)
    return jnp.concatenate(
        [dot(squares[:, :256], averaging), dot(squares[:, 256:], averaging)], axis=1
    )


def queries(state, gain, probe, averaging):
    mean_square = jnp.mean(state * state, axis=-1, keepdims=True)
    raw = dot((state * gain).astype(bf16), probe)
    return (raw * lax.rsqrt(head_mean(raw, averaging) + eps * (mean_square + eps))).astype(bf16)


def normalize(values, gain):
    return values * lax.rsqrt(jnp.mean(values * values, axis=-1, keepdims=True) + eps) * gain


def score_scale(scales, tier):
    lane_head = iota((1, width), 1) // head
    row = jnp.zeros((1, width), f32)
    for h in range(heads):
        row = jnp.where(lane_head == h, scales[tier, h], row)
    return row * (log2e / math.sqrt(head))


def keys_values(latents, tier, expand, shrink, address, content, gains, scales, averaging):
    base = latents.astype(f32)
    hidden = dot(normalize(base, gains[tier, 1:2, :]).astype(bf16), expand)
    hidden = (hidden * (0.5 + 0.5 * jnp.tanh(0.5 * hidden))).astype(bf16)
    renewed = (base + dot(hidden, shrink)).astype(bf16).astype(f32)
    kv_in = normalize(renewed, gains[tier, 2:3, :]).astype(bf16)
    key_part = dot(kv_in, address)
    key_part = key_part * lax.rsqrt(head_mean(key_part, averaging) + eps)
    key_part = (key_part * score_scale(scales, tier)).astype(bf16)
    return key_part, dot(kv_in, content).astype(bf16)


def log_counts(places, rows):
    blocks = places.shape[0]
    doubled = jnp.concatenate([places, places], axis=0).astype(f32).astype(bf16)
    eye = (iota((listed, listed), 0) == iota((listed, listed), 1)).astype(f32).astype(bf16)
    turned = dot_t(eye, doubled)
    latent = iota((rows, 2 * blocks), 0).astype(f32)
    count = jnp.zeros((rows, 2 * blocks), f32)
    for j in range(listed):
        count = count + jnp.where(turned[j : j + 1, :] == latent, 1.0, 0.0)
    logs = jnp.where(count > 0.5, jnp.log(jnp.maximum(count, 1.0)) * log2e, masked)
    high = logs.astype(bf16).astype(f32)
    lane = iota((rows, 2 * blocks), 1)
    return jnp.where(lane < blocks, high, logs - high).astype(bf16)


def block_onehot(first_row, rows, blocks, per_block):
    block = (iota((rows, 2 * blocks), 0) + first_row) // per_block
    return (block == iota((rows, 2 * blocks), 1) % blocks).astype(f32).astype(bf16)


def first_queries_kernel(x_hbm, probe_hbm, gains, q_ref, x_buf, probe_buf, sems):
    rows = x_buf.shape[0]
    steps = rows // tile
    copies = [pltpu.make_async_copy(probe_hbm.at[0], probe_buf, sems.at[steps])]
    for t in range(steps):
        part = pl.ds(t * tile, tile)
        copies.append(pltpu.make_async_copy(x_hbm.at[part], x_buf.at[part], sems.at[t]))
    for copy in copies:
        copy.start()
    averaging = head_mean_matrix()
    copies[0].wait()
    for t in range(steps):
        copies[t + 1].wait()
        part = pl.ds(t * tile, tile)
        q_ref[part, :] = queries(
            x_buf[part, :].astype(f32), gains[0, 0:1, :], probe_buf[...], averaging
        )


def first_queries(x, probe, gains):
    rows = x.shape[0]
    return pl.pallas_call(
        first_queries_kernel,
        name="first_queries",
        out_shape=jax.ShapeDtypeStruct((rows, width), bf16),
        in_specs=[anywhere, anywhere, in_vmem],
        out_specs=in_vmem,
        scratch_shapes=[
            pltpu.VMEM((rows, width), bf16),
            pltpu.VMEM((width, width), bf16),
            pltpu.SemaphoreType.DMA((rows // tile + 1,)),
        ],
        cost_estimate=pl.CostEstimate(
            flops=2 * rows * width * width * 2, bytes_accessed=4 << 20, transcendentals=rows * width
        ),
    )(x, probe, gains)


def first_table_kernel(
    low, own, high, expand, shrink, address, content, gains, scales, k_ref, v_ref, e, s, a, c, sems
):
    copies = [
        pltpu.make_async_copy(source.at[0], target, sems.at[i])
        for i, (source, target) in enumerate(
            ((expand, e), (shrink, s), (address, a), (content, c))
        )
    ]
    for copy in copies:
        copy.start()
    averaging = head_mean_matrix()
    latents = jnp.concatenate([low[...], own[...], high[...]], axis=0)
    for copy in copies:
        copy.wait()
    k_ref[...], v_ref[...] = keys_values(
        latents, 0, e[...], s[...], a[...], c[...], gains, scales, averaging
    )


def first_table(low, own, high, expand, shrink, address, content, gains, scales):
    rows = 3 * own.shape[0]
    hidden = expand.shape[2]
    return pl.pallas_call(
        first_table_kernel,
        name="first_table",
        out_shape=[jax.ShapeDtypeStruct((rows, width), bf16)] * 2,
        in_specs=[in_vmem] * 3 + [anywhere] * 4 + [in_vmem, in_smem],
        out_specs=[in_vmem] * 2,
        scratch_shapes=[
            pltpu.VMEM((width, hidden), bf16),
            pltpu.VMEM((hidden, width), bf16),
            pltpu.VMEM((width, width), bf16),
            pltpu.VMEM((width, width), bf16),
            pltpu.SemaphoreType.DMA((4,)),
        ],
        cost_estimate=pl.CostEstimate(
            flops=16 * rows * width * hidden, bytes_accessed=8 << 20, transcendentals=rows * hidden
        ),
    )(low, own, high, expand, shrink, address, content, gains, scales)


def first_mix_kernel(
    first_row, x_hbm, q_ref, k_ref, v_ref, picks, merge_hbm, s_ref, x_buf, merge, kx, vx, sems
):
    rows = s_ref.shape[0]
    table = k_ref.shape[0]
    blocks = picks.shape[0]
    copies = [
        pltpu.make_async_copy(x_hbm.at[pl.ds(first_row, rows)], x_buf, sems.at[0]),
        pltpu.make_async_copy(merge_hbm.at[0], merge, sems.at[1]),
    ]
    for copy in copies:
        copy.start()
    listing = picks[...]
    local = listing - listing[:, 0:1] + iota(listing.shape, 0) + blocks
    logs = log_counts(local, table)
    lane = iota((table, 128), 1)
    zero = jnp.zeros((table, 128), bf16)
    left = jnp.where(lane < head, 1.0, 0.0).astype(bf16)
    right = jnp.where(lane >= head, 1.0, 0.0).astype(bf16)
    for p in range(heads // 2):
        lanes = slice(128 * p, 128 * p + 128)
        k, v = k_ref[:, lanes], v_ref[:, lanes]
        for i, side in enumerate((left, right)):
            part = pl.ds(i * table, table)
            kx[p, part, 0:128] = jnp.where(side > zero, k, zero)
            kx[p, part, 128:256] = logs
            vx[p, part, 0:128] = jnp.where(side > zero, v, zero)
            vx[p, part, 128:256] = side
    for copy in copies:
        copy.wait()

    def step(t, carry):
        part = pl.ds(pl.multiple_of(t * tile, tile), tile)
        onehot = block_onehot(first_row + t * tile, tile, blocks, 16)
        mixed = []
        for p in range(heads // 2):
            q = q_ref[pl.ds(pl.multiple_of(first_row + t * tile, tile), tile), 128 * p : 128 * p + 128]
            scores = dot_t(jnp.concatenate([q, onehot], axis=1), kx[p])
            sums = dot(jnp.exp2(scores).astype(bf16), vx[p])
            mixed.append((sums[:, :128] / sums[:, 128:]).astype(bf16))
        s_ref[part, :] = x_buf[part, :].astype(f32) + dot(
            jnp.concatenate(mixed, axis=1), merge[...]
        )
        return carry

    lax.fori_loop(0, rows // tile, step, 0)


def first_mix(x, q, k, v, picks, merge, first_row, rows):
    table = k.shape[0]
    return pl.pallas_call(
        functools.partial(first_mix_kernel, first_row),
        name="first_mix",
        out_shape=jax.ShapeDtypeStruct((rows, width), f32),
        in_specs=[anywhere, in_vmem, in_vmem, in_vmem, in_vmem, anywhere],
        out_specs=in_vmem,
        scratch_shapes=[
            pltpu.VMEM((rows, width), bf16),
            pltpu.VMEM((width, width), bf16),
            pltpu.VMEM((heads // 2, 2 * table, 256), bf16),
            pltpu.VMEM((heads // 2, 2 * table, 256), bf16),
            pltpu.SemaphoreType.DMA((2,)),
        ],
        cost_estimate=pl.CostEstimate(
            flops=rows * width * width * 14, bytes_accessed=4 << 20, transcendentals=rows * 1536
        ),
    )(x, q, k, v, picks, merge)


def coarse_kernel(
    state_a,
    state_b,
    tables,
    picks_two,
    picks_three,
    place,
    probe_hbm,
    address_hbm,
    content_hbm,
    merge_hbm,
    expand_hbm,
    shrink_hbm,
    gains,
    scales,
    out_ref,
    probe,
    address,
    content,
    merge,
    expand,
    shrink,
    kx,
    vm,
    sems,
):
    blocks = picks_two.shape[0]
    latents = tables.shape[1]
    half = state_a.shape[0]
    columns = heads * latents
    copies = []
    for i in range(2):
        for j, (source, target) in enumerate(
            (
                (expand_hbm, expand),
                (shrink_hbm, shrink),
                (address_hbm, address),
                (content_hbm, content),
                (merge_hbm, merge),
                (probe_hbm, probe),
            )
        ):
            copies.append(
                pltpu.make_async_copy(source.at[i + 1], target.at[i], sems.at[6 * i + j])
            )
    for copy in copies:
        copy.start()
    averaging = head_mean_matrix()
    group, core = place[0, 0], place[0, 1]
    two = (picks_two[...] & (latents - 1)) ^ (group << 2)
    raw = picks_three[...]
    source_group = ((raw >> 2) & 3) * 2 + (raw >> 4)
    three = ((source_group ^ group) << 2) | ((raw & 3) ^ (core << 1))
    own_head = iota((columns, width), 0) // latents == iota((columns, width), 1) // head
    zero = jnp.zeros((columns, width), bf16)
    for i, places in enumerate((two, three)):
        logs = log_counts(places, latents)
        for copy in copies[6 * i : 6 * i + 5]:
            copy.wait()
        k, v = keys_values(
            tables[i], i + 1, expand[i], shrink[i], address[i], content[i], gains, scales, averaging
        )
        kx[i, :, 0:width] = jnp.where(own_head, jnp.concatenate([k] * heads, axis=0), zero)
        kx[i, :, width : width + 128] = jnp.concatenate([logs] * heads, axis=0)
        vm[i] = dot(
            jnp.where(own_head, jnp.concatenate([v] * heads, axis=0), zero), merge[i]
        ).astype(bf16)
    copies[5].wait()
    copies[11].wait()
    same = iota((columns, columns), 0) // latents == iota((columns, columns), 1) // latents
    summing = jnp.where(same, 1.0, 0.0).astype(bf16)

    for n, state_ref in enumerate((state_a, state_b)):

        def step(t, carry, n=n, state_ref=state_ref):
            part = pl.ds(pl.multiple_of(t * tile, tile), tile)
            onehot = block_onehot(n * half + t * tile, tile, blocks, 16)
            state = state_ref[part, :]
            for i in range(2):
                q = queries(state, gains[i + 1, 0:1, :], probe[i], averaging)
                scores = dot_t(jnp.concatenate([q, onehot], axis=1), kx[i])
                powers = jnp.exp2(scores)
                weights = (powers / dot(powers.astype(bf16), summing)).astype(bf16)
                state = state + dot(weights, vm[i])
            out_ref[pl.ds(pl.multiple_of(n * half + t * tile, tile), tile), :] = state.astype(bf16)
            return carry

        lax.fori_loop(0, half // tile, step, 0)


def coarse(
    state_a, state_b, tables, two, three, place, probe, address, content, merge, expand, shrink, gains, scales
):
    rows = 2 * state_a.shape[0]
    hidden = expand.shape[2]
    columns = heads * tables.shape[1]
    square = pltpu.VMEM((2, width, width), bf16)
    return pl.pallas_call(
        coarse_kernel,
        name="coarse",
        out_shape=jax.ShapeDtypeStruct((rows, width), bf16),
        in_specs=[in_vmem] * 5 + [in_smem] + [anywhere] * 6 + [in_vmem, in_smem],
        out_specs=in_vmem,
        scratch_shapes=[
            square,
            square,
            square,
            square,
            pltpu.VMEM((2, width, hidden), bf16),
            pltpu.VMEM((2, hidden, width), bf16),
            pltpu.VMEM((2, columns, width + 128), bf16),
            pltpu.VMEM((2, columns, width), bf16),
            pltpu.SemaphoreType.DMA((12,)),
        ],
        cost_estimate=pl.CostEstimate(
            flops=rows * width * width * 12, bytes_accessed=12 << 20, transcendentals=rows * 2048
        ),
    )(
        state_a, state_b, tables, two, three, place, probe, address, content, merge, expand, shrink, gains, scales
    )


def turn_pairs(flip):
    pairs = []
    for y_hi in range(2):
        for x in range(4):
            for core in range(2):
                for z in range(4):
                    for y_lo in range(2):
                        target = (y_hi * 8 + x * 2 + core) * 8 + z * 2 + y_lo
                        source = (y_lo * 8 + z * 2 + (core ^ flip)) * 8 + x * 2 + y_hi
                        pairs.append((source, target))
    return pairs


def per_device(
    pixel_features,
    tier_one_codes,
    tier_two_codes,
    tier_three_codes,
    tier_one_picks,
    tier_two_picks,
    tier_three_picks,
    probe_matrix,
    address_matrix,
    content_matrix,
    merge_matrix,
    expand_matrix,
    shrink_matrix,
    rescale_factors,
    logit_scaling,
):
    devices = lax.axis_size(both)
    members = lax.axis_size("grp")
    forward = [(i, i + 1) for i in range(devices - 1)]
    backward = [(i + 1, i) for i in range(devices - 1)]
    low = lax.ppermute(tier_one_codes, both, forward)
    high = lax.ppermute(tier_one_codes, both, backward)
    near = lax.ppermute(tier_three_codes, both, turn_pairs(0))
    far = lax.ppermute(tier_three_codes, both, turn_pairs(1))
    q = first_queries(pixel_features, probe_matrix, rescale_factors)
    tables = jnp.stack([tier_two_codes, jnp.concatenate([near, far], axis=0)], axis=0)
    for k in (1, 2, 4):
        tables = jnp.concatenate(
            [tables, lax.ppermute(tables, "grp", [(i, i ^ k) for i in range(members)])], axis=1
        )
    k, v = first_table(
        low,
        tier_one_codes,
        high,
        expand_matrix,
        shrink_matrix,
        address_matrix,
        content_matrix,
        rescale_factors,
        logit_scaling,
    )
    half = pixel_features.shape[0] // 2
    state_a = first_mix(pixel_features, q, k, v, tier_one_picks, merge_matrix, 0, half)
    state_b = first_mix(pixel_features, q, k, v, tier_one_picks, merge_matrix, half, half)
    place = jnp.stack([lax.axis_index("grp"), lax.axis_index("sph") % 2]).reshape(1, 2)
    return coarse(
        state_a,
        state_b,
        tables,
        tier_two_picks,
        tier_three_picks,
        place.astype(jnp.int32),
        probe_matrix,
        address_matrix,
        content_matrix,
        merge_matrix,
        expand_matrix,
        shrink_matrix,
        rescale_factors,
        logit_scaling,
    )


def solution(mesh):
    placed = (
        P(both, None),
        P(both, None),
        P(both, None),
        P("sph", None),
        P(both, None),
        P(both, None),
        P(both, None),
        P(),
        P(),
        P(),
        P(),
        P(),
        P(),
        P(),
        P(),
    )
    return jax.shard_map(
        per_device, mesh=mesh, in_specs=placed, out_specs=P(both, None), check_vma=False
    )
```
